32 devices in a mesh: groups: 2 (over y), blk: 4 (over z), tile: 2 (over x), pair: 2 (over core).
Axes of the slice: x: 2, y: 2, z: 4, core: 2. Of those that a mesh axis runs over, the one named last changes fastest.
Arguments:
- left_tokens: bfloat16 [4, 1536, 768], P(('groups', 'pair'), 'blk', 'tile'), parts along dimension 0, may hold values from -32 to 32
- right_tokens: bfloat16 [4, 1536, 768], P(('groups', 'pair'), 'blk', 'tile'), parts along dimension 0, may hold values from -32 to 32
- self_qkv: bfloat16 [3, 768, 512], P(None, None, 'tile'), may hold values from -1 to 1
- self_out: bfloat16 [512, 768], P('tile'), may hold values from -0.25 to 0.25
- cross_qkv: bfloat16 [3, 768, 512], P(None, None, 'tile'), may hold values from -1 to 1
- cross_out: bfloat16 [512, 768], P('tile'), may hold values from -0.25 to 0.25
- reassemble: bfloat16 [768, 256], P('tile'), may hold values from -0.21875 to 0.21875
- conv_weight: bfloat16 [3, 3, 256, 256], replicated, may hold values from -0.125 to 0.125
Outputs:
- joined: bfloat16 [4, 12, 128, 256], P(('groups', 'pair'), 'blk', 'tile'), parts along dimension 0
The draws below stay inside these ranges and needn't reach their ends.
There are 2 independent parts, one for each index of `groups`. The reference program is written for one: setup_inputs(seed, part) draws one part's arguments, and reference() takes and returns one part's arrays. A program takes and returns all parts, laid end to end along the dimension named above; an argument that names none is the same for every part. Nothing has to cross between parts.
All inputs are finite; a program needn't handle non-finite values.
Results may differ from the reference program's by a relative error of at most 0.018.
Values may be sent and summed in bfloat16 or wider, within the bound.
A program may use at most 64 MiB of HBM per device.

```python
import math
import jax
import jax.numpy as jnp
from jax import lax

D = 768
HEADS = 8
HD = 64
CH = 256
GRID_W = 128
PAIRS = 2
GRID_H = 12
LEN = 1536


def token_field(key):
    keys = jax.random.split(key, 3)
    noise = jax.random.truncated_normal(keys[0], -4.0, 4.0, (PAIRS, LEN, D), jnp.float32)
    row_scale = jnp.exp(jax.random.uniform(keys[1], (PAIRS, LEN, 1), jnp.float32, math.log(0.3), math.log(3.0)))
    column_scale = jnp.exp(jax.random.uniform(keys[2], (D,), jnp.float32, math.log(0.2), math.log(2.0)))
    field = noise * column_scale
    return (field * row_scale).astype(jnp.bfloat16)


def projection_weights(key):
    keys = jax.random.split(key, 1)
    columns = HEADS * HD
    scales = jnp.array([1.67, 1.67, 1.0], jnp.float32)[:, None, None] / math.sqrt(D)
    weights = jax.random.truncated_normal(keys[0], -4.0, 4.0, (3, D, columns), jnp.float32) * scales
    return weights.astype(jnp.bfloat16)


def draw_left_tokens(key, part):
    return token_field(jax.random.fold_in(key, 3))


def draw_right_tokens(key, part):
    return token_field(jax.random.fold_in(key, 11))


def draw_self_qkv(key, part):
    return projection_weights(jax.random.fold_in(key, 19))


def draw_cross_qkv(key, part):
    return projection_weights(jax.random.fold_in(key, 29))


def steps_of(rng, shape, pieces, least, largest):
    factor_of = 1.0
    for position, shards_of in pieces:
        draws = jax.random.uniform(jax.random.fold_in(jax.random.fold_in(rng, 6), position), (shards_of,), jnp.float32, least / len(pieces), largest / len(pieces))
        factor_of = factor_of * jnp.repeat(jnp.exp(draws), shape[position] // shards_of).reshape((-1,) + (1,) * (len(shape) - 1 - position))
    return factor_of


def gaussian(key, dims, width, reach, shards=(), held_as=jnp.bfloat16):
    entries = jax.random.normal(key, dims, jnp.float32) * width
    if len(shards) > 0:
        entries = steps_of(key, dims, shards, -0.22, 0.18) * entries
    return jnp.clip(entries, min=-reach, max=reach).astype(held_as)


def setup_inputs(seed: int = 0, part: int = 0) -> dict:
    key_of = jax.random.split(jax.random.key(seed), 9)
    part_keys = jax.random.split(jax.random.fold_in(key_of[8], part), 9)
    return {
        "left_tokens": draw_left_tokens(jax.random.fold_in(jax.random.fold_in(key_of[8], part), 71), part),
        "right_tokens": draw_right_tokens(jax.random.fold_in(jax.random.fold_in(key_of[8], part), 71), part),
        "self_qkv": draw_self_qkv(jax.random.fold_in(key_of[8], 71), part),
        "self_out": gaussian(key_of[3], (HEADS * HD, D), (HEADS * HD) ** -0.5, 0.25, ((0, 2),)),
        "cross_qkv": draw_cross_qkv(jax.random.fold_in(key_of[8], 71), part),
        "cross_out": gaussian(key_of[5], (HEADS * HD, D), (HEADS * HD) ** -0.5, 0.25, ((0, 2),)),
        "reassemble": gaussian(key_of[6], (D, CH), D ** -0.5, 0.21875, ((0, 2),)),
        "conv_weight": gaussian(key_of[7], (3, 3, CH, CH), (9 * CH) ** -0.5, 0.125),
    }


def layer_norm(values):
    widened = values.astype(jnp.float32)
    centred = widened - lax.optimization_barrier(jnp.mean(widened, axis=-1, keepdims=True))
    variance = lax.optimization_barrier(jnp.mean(centred * centred, axis=-1, keepdims=True))
    return (centred * lax.rsqrt(variance + 1e-06)).astype(jnp.bfloat16)

def project_rows(normed, weight):
    return jnp.dot(normed, weight, preferred_element_type=jnp.float32).astype(jnp.bfloat16)

def attention(queries, keys_rows, values_rows):
    block_rows = math.gcd(LEN, 512)
    query_blocks = queries.reshape(LEN // block_rows, block_rows, HEADS, HD)
    keys_wide = keys_rows.reshape(LEN, HEADS, HD).astype(jnp.float32)
    values_wide = values_rows.reshape(LEN, HEADS, HD).astype(jnp.float32)

    def one_block(query_block):
        scores = jnp.einsum('qhd,khd->hqk', query_block.astype(jnp.float32), keys_wide) * HD ** (-0.5)
        maxima = lax.optimization_barrier(jnp.max(scores, axis=2, keepdims=True))
        expanded = jnp.exp(scores - maxima)
        totals = lax.optimization_barrier(jnp.sum(expanded, axis=2))
        rounded = lax.optimization_barrier(expanded.astype(jnp.bfloat16)).astype(jnp.float32)
        mixed = jnp.einsum('hqk,khd->qhd', rounded, values_wide)
        return (mixed / totals.T[:, :, None]).reshape(block_rows, HEADS * HD).astype(jnp.bfloat16)
    return lax.map(one_block, query_blocks).reshape(LEN, HEADS * HD)

def one_pair(left_rows, right_rows, self_qkv, self_out, cross_qkv, cross_out, reassemble, conv_weight):
    left_normed = layer_norm(left_rows)
    right_normed = layer_norm(right_rows)
    self_mixed = attention(project_rows(left_normed, self_qkv[0]), project_rows(left_normed, self_qkv[1]), project_rows(left_normed, self_qkv[2]))
    updated = (left_rows.astype(jnp.float32) + jnp.dot(self_mixed, self_out, preferred_element_type=jnp.float32)).astype(jnp.bfloat16)
    updated_normed = layer_norm(updated)
    cross_mixed = attention(project_rows(updated_normed, cross_qkv[0]), project_rows(right_normed, cross_qkv[1]), project_rows(right_normed, cross_qkv[2]))
    final_tokens = (updated.astype(jnp.float32) + jnp.dot(cross_mixed, cross_out, preferred_element_type=jnp.float32)).astype(jnp.bfloat16)
    feature_map = jnp.dot(final_tokens, reassemble, preferred_element_type=jnp.float32).astype(jnp.bfloat16).reshape(GRID_H, GRID_W, CH)
    activated = jnp.maximum(feature_map, jnp.zeros((), jnp.bfloat16))
    padded = jnp.pad(activated, ((1, 1), (1, 1), (0, 0)))
    stacked = jnp.concatenate([padded[row_shift:row_shift + GRID_H, col_shift:col_shift + GRID_W] for row_shift in range(3) for col_shift in range(3)], axis=-1)
    convolved = jnp.dot(stacked.reshape(GRID_H * GRID_W, 9 * CH), conv_weight.reshape(9 * CH, CH), preferred_element_type=jnp.float32)
    return (feature_map.astype(jnp.float32) + convolved.reshape(GRID_H, GRID_W, CH)).astype(jnp.bfloat16)

def reference(left_tokens, right_tokens, self_qkv, self_out, cross_qkv, cross_out, reassemble, conv_weight):
    results = [one_pair(left_tokens[index], right_tokens[index], self_qkv, self_out, cross_qkv, cross_out, reassemble, conv_weight) for index in range(PAIRS)]
    return jnp.stack(results, axis=0)
```

```python
import jax
import jax.numpy as jnp
from jax import lax
from jax.sharding import PartitionSpec as P

HD = 64
CH = 256
GRID_W = 128


def padded_2(cells, sides, width):
    for axis, dim in sides:
        count = lax.axis_size(axis)
        ends = count - 1
        head = lax.slice_in_dim(cells, 0, width, axis=dim)
        tail = lax.slice_in_dim(cells, cells.shape[dim] - width, cells.shape[dim], axis=dim)
        cells = jnp.concatenate(
            [
                lax.ppermute(tail, axis, [(i, (i + 1) % count) for i in range(ends)]),
                cells,
                lax.ppermute(head, axis, [((i + 1) % count, i) for i in range(ends)]),
            ],
            axis=dim,
        )
    return cells


def layer_norm(values):
    widened = values.astype(jnp.float32)
    centred = widened - jnp.mean(widened, axis=-1, keepdims=True)
    variance = jnp.mean(centred * centred, axis=-1, keepdims=True)
    return (centred * lax.rsqrt(variance + 1e-06)).astype(jnp.bfloat16)


def project_rows(normed, weight):
    return jnp.dot(normed, weight, preferred_element_type=jnp.float32).astype(jnp.bfloat16)


def initial_state(queries):
    query_count = queries.shape[0]
    head_count = queries.shape[1] // HD
    return (
        jnp.full((head_count, query_count), -1e30, jnp.float32),
        jnp.zeros((head_count, query_count), jnp.float32),
        jnp.zeros(queries.shape, jnp.float32),
    )


def attend_keys(running, queries, keys_rows, values_rows):
    maxima, totals, accumulated = running
    query_count = queries.shape[0]
    head_count = queries.shape[1] // HD
    key_count = keys_rows.shape[0]
    scores = jnp.einsum(
        "qhd,khd->hqk",
        queries.reshape(query_count, head_count, HD),
        keys_rows.reshape(key_count, head_count, HD),
        preferred_element_type=jnp.float32,
    ) * HD ** (-0.5)
    new_maxima = jnp.maximum(maxima, jnp.max(scores, axis=2))
    correction = jnp.exp(maxima - new_maxima)
    expanded = jnp.exp(scores - new_maxima[:, :, None])
    totals = totals * correction + jnp.sum(expanded, axis=2)
    mixed = jnp.einsum(
        "hqk,khd->qhd",
        expanded.astype(jnp.bfloat16),
        values_rows.reshape(key_count, head_count, HD),
        preferred_element_type=jnp.float32,
    )
    accumulated = (
        accumulated.reshape(query_count, head_count, HD) * correction.T[:, :, None] + mixed
    )
    return (new_maxima, totals, accumulated.reshape(query_count, head_count * HD))


def fold_keys(running, queries, keys_rows, values_rows):
    key_count = keys_rows.shape[0]
    block_rows = max((divisor for divisor in range(1, 1025) if key_count % divisor == 0))
    if block_rows == key_count:
        return attend_keys(running, queries, keys_rows, values_rows)
    stacked_keys = keys_rows.reshape(key_count // block_rows, block_rows, keys_rows.shape[1])
    stacked_values = values_rows.reshape(key_count // block_rows, block_rows, values_rows.shape[1])

    def step_block(current, blocks):
        return (attend_keys(current, queries, blocks[0], blocks[1]), None)

    result, unused = lax.scan(step_block, running, (stacked_keys, stacked_values))
    return result


def finish_state(running):
    maxima, totals, accumulated = running
    query_count = accumulated.shape[0]
    head_count = accumulated.shape[1] // HD
    normalized = accumulated.reshape(query_count, head_count, HD) / totals.T[:, :, None]
    return normalized.reshape(query_count, head_count * HD).astype(jnp.bfloat16)


def body(
    left_tokens, right_tokens, self_qkv, self_out, cross_qkv, cross_out, reassemble, conv_weight
):
    tiles = lax.axis_size("tile")
    tile_index = lax.axis_index("tile")
    token_count, feature_share = left_tokens.shape[1], left_tokens.shape[2]
    packed = jnp.concatenate(
        [left_tokens[0].reshape(-1), right_tokens[0].reshape(-1), reassemble.reshape(-1)]
    )
    gathered = lax.all_gather(packed, "tile", axis=0)
    block = token_count * feature_share

    def features(offset):
        return jnp.concatenate(
            [gathered[i, offset : offset + block].reshape(token_count, feature_share) for i in range(tiles)],
            axis=1,
        )

    left_full = features(0)
    right_full = features(block)
    reassemble_full = gathered[:, 2 * block :].reshape(tiles * reassemble.shape[0], CH)
    left_normed = layer_norm(left_full)
    right_normed = layer_norm(right_full)
    self_query = project_rows(left_normed, self_qkv[0])
    projected = jnp.stack(
        [
            project_rows(left_normed, self_qkv[1]),
            project_rows(left_normed, self_qkv[2]),
            project_rows(right_normed, cross_qkv[1]),
            project_rows(right_normed, cross_qkv[2]),
        ]
    )
    pieces = lax.all_gather(projected, "blk", axis=1, tiled=True)
    self_state = fold_keys(initial_state(self_query), self_query, pieces[0], pieces[1])
    self_mixed = finish_state(self_state)
    self_term = jnp.dot(self_mixed, self_out, preferred_element_type=jnp.float32)
    self_sum = lax.psum(self_term.astype(jnp.bfloat16), "tile").astype(jnp.float32)
    updated = (left_full.astype(jnp.float32) + self_sum).astype(jnp.bfloat16)
    updated_normed = layer_norm(updated)
    cross_query = project_rows(updated_normed, cross_qkv[0])
    cross_state = fold_keys(initial_state(cross_query), cross_query, pieces[2], pieces[3])
    cross_mixed = finish_state(cross_state)
    cross_term = jnp.dot(cross_mixed, cross_out, preferred_element_type=jnp.float32)
    cross_sum = lax.psum(cross_term.astype(jnp.bfloat16), "tile").astype(jnp.float32)
    final_tokens = (updated.astype(jnp.float32) + cross_sum).astype(jnp.bfloat16)
    band_rows = token_count // GRID_W
    column_count = GRID_W // tiles
    grid = jnp.pad(final_tokens.reshape(band_rows, GRID_W, -1), ((0, 0), (1, 1), (0, 0)))
    window = lax.dynamic_slice_in_dim(grid, tile_index * column_count, column_count + 2, axis=1)
    wide_map = (
        jnp.dot(
            window.reshape(band_rows * (column_count + 2), -1),
            reassemble_full,
            preferred_element_type=jnp.float32,
        )
        .astype(jnp.bfloat16)
        .reshape(band_rows, column_count + 2, CH)
    )
    feature_map = wide_map[:, 1 : column_count + 1]
    activated = jnp.maximum(wide_map, jnp.zeros((), jnp.bfloat16))
    padded = padded_2(activated, (("blk", 0),), 1)
    stacked = jnp.concatenate(
        [
            padded[row_shift : row_shift + band_rows, col_shift : col_shift + column_count]
            for row_shift in range(3)
            for col_shift in range(3)
        ],
        axis=-1,
    )
    convolved = jnp.dot(
        stacked.reshape(band_rows * column_count, 9 * CH),
        conv_weight.reshape(9 * CH, CH),
        preferred_element_type=jnp.float32,
    )
    joined = (
        feature_map.astype(jnp.float32) + convolved.reshape(band_rows, column_count, CH)
    ).astype(jnp.bfloat16)
    return joined[None]


def solution(mesh):
    placed = (
        P(("groups", "pair"), "blk", "tile"),
        P(("groups", "pair"), "blk", "tile"),
        P(None, None, "tile"),
        P("tile", None),
        P(None, None, "tile"),
        P("tile", None),
        P("tile", None),
        P(),
    )
    return jax.shard_map(
        body,
        mesh=mesh,
        in_specs=placed,
        out_specs=P(("groups", "pair"), "blk", "tile", None),
        check_vma=False,
    )
```

```python
import jax
import jax.numpy as jnp
from jax import lax
from jax.sharding import PartitionSpec as P

HD = 64
CH = 256
GRID_W = 128


def padded_2(cells, sides, width):
    for axis, dim in sides:
        count = lax.axis_size(axis)
        ends = count - 1
        head = lax.slice_in_dim(cells, 0, width, axis=dim)
        tail = lax.slice_in_dim(cells, cells.shape[dim] - width, cells.shape[dim], axis=dim)
        cells = jnp.concatenate(
            [
                lax.ppermute(tail, axis, [(i, (i + 1) % count) for i in range(ends)]),
                cells,
                lax.ppermute(head, axis, [((i + 1) % count, i) for i in range(ends)]),
            ],
            axis=dim,
        )
    return cells


def layer_norm(values):
    widened = values.astype(jnp.float32)
    centred = widened - jnp.mean(widened, axis=-1, keepdims=True)
    variance = jnp.mean(centred * centred, axis=-1, keepdims=True)
    return (centred * lax.rsqrt(variance + 1e-06)).astype(jnp.bfloat16)


def project_rows(normed, weight):
    return jnp.dot(normed, weight, preferred_element_type=jnp.float32).astype(jnp.bfloat16)


def initial_state(queries):
    query_count = queries.shape[0]
    head_count = queries.shape[1] // HD
    return (
        jnp.full((head_count, query_count), -1e30, jnp.float32),
        jnp.zeros((head_count, query_count), jnp.float32),
        jnp.zeros(queries.shape, jnp.float32),
    )


def attend_keys(running, queries, keys_rows, values_rows):
    maxima, totals, accumulated = running
    query_count = queries.shape[0]
    head_count = queries.shape[1] // HD
    key_count = keys_rows.shape[0]
    scores = jnp.einsum(
        "qhd,khd->hqk",
        queries.reshape(query_count, head_count, HD),
        keys_rows.reshape(key_count, head_count, HD),
        preferred_element_type=jnp.float32,
    ) * HD ** (-0.5)
    new_maxima = jnp.maximum(maxima, jnp.max(scores, axis=2))
    correction = jnp.exp(maxima - new_maxima)
    expanded = jnp.exp(scores - new_maxima[:, :, None])
    totals = totals * correction + jnp.sum(expanded, axis=2)
    mixed = jnp.einsum(
        "hqk,khd->qhd",
        expanded.astype(jnp.bfloat16),
        values_rows.reshape(key_count, head_count, HD),
        preferred_element_type=jnp.float32,
    )
    accumulated = (
        accumulated.reshape(query_count, head_count, HD) * correction.T[:, :, None] + mixed
    )
    return (new_maxima, totals, accumulated.reshape(query_count, head_count * HD))


def fold_keys(running, queries, keys_rows, values_rows):
    key_count = keys_rows.shape[0]
    block_rows = max((divisor for divisor in range(1, 1025) if key_count % divisor == 0))
    if block_rows == key_count:
        return attend_keys(running, queries, keys_rows, values_rows)
    stacked_keys = keys_rows.reshape(key_count // block_rows, block_rows, keys_rows.shape[1])
    stacked_values = values_rows.reshape(key_count // block_rows, block_rows, values_rows.shape[1])

    def step_block(current, blocks):
        return (attend_keys(current, queries, blocks[0], blocks[1]), None)

    result, unused = lax.scan(step_block, running, (stacked_keys, stacked_values))
    return result


def finish_state(running):
    maxima, totals, accumulated = running
    query_count = accumulated.shape[0]
    head_count = accumulated.shape[1] // HD
    normalized = accumulated.reshape(query_count, head_count, HD) / totals.T[:, :, None]
    return normalized.reshape(query_count, head_count * HD).astype(jnp.bfloat16)


def shifted(value, axis):
    count = lax.axis_size(axis)
    return [value] + [
        lax.ppermute(value, axis, [(i, (i + shift) % count) for i in range(count)])
        for shift in range(1, count)
    ]


def gather_ordered(value, axis):
    count = lax.axis_size(axis)
    stack = jnp.stack(shifted(value, axis))
    order = (lax.axis_index(axis) - jnp.arange(count)) % count
    return jnp.take(stack, order, axis=0)


def sum_over(value, axis):
    total = value.astype(jnp.float32)
    for piece in shifted(value, axis)[1:]:
        total = total + piece.astype(jnp.float32)
    return total


def body(
    left_tokens, right_tokens, self_qkv, self_out, cross_qkv, cross_out, reassemble, conv_weight
):
    tiles = lax.axis_size("tile")
    tile_index = lax.axis_index("tile")
    token_count, feature_share = left_tokens.shape[1], left_tokens.shape[2]
    tokens = gather_ordered(jnp.stack([left_tokens[0], right_tokens[0]]), "tile")
    left_full, right_full = (
        jnp.moveaxis(tokens[:, side], 0, 1).reshape(token_count, tiles * feature_share)
        for side in range(2)
    )
    reassemble_full = gather_ordered(reassemble, "tile").reshape(-1, CH)
    left_normed = layer_norm(left_full)
    right_normed = layer_norm(right_full)
    self_query = project_rows(left_normed, self_qkv[0])
    projected = jnp.stack(
        [
            project_rows(left_normed, self_qkv[1]),
            project_rows(left_normed, self_qkv[2]),
            project_rows(right_normed, cross_qkv[1]),
            project_rows(right_normed, cross_qkv[2]),
        ]
    )
    pieces = jnp.concatenate(shifted(projected, "blk"), axis=1)
    self_state = fold_keys(initial_state(self_query), self_query, pieces[0], pieces[1])
    self_mixed = finish_state(self_state)
    self_term = jnp.dot(self_mixed, self_out, preferred_element_type=jnp.float32)
    self_sum = sum_over(self_term.astype(jnp.bfloat16), "tile")
    updated = (left_full.astype(jnp.float32) + self_sum).astype(jnp.bfloat16)
    updated_normed = layer_norm(updated)
    cross_query = project_rows(updated_normed, cross_qkv[0])
    cross_state = fold_keys(initial_state(cross_query), cross_query, pieces[2], pieces[3])
    cross_mixed = finish_state(cross_state)
    cross_term = jnp.dot(cross_mixed, cross_out, preferred_element_type=jnp.float32)
    cross_sum = sum_over(cross_term.astype(jnp.bfloat16), "tile")
    final_tokens = (updated.astype(jnp.float32) + cross_sum).astype(jnp.bfloat16)
    band_rows = token_count // GRID_W
    column_count = GRID_W // tiles
    grid = jnp.pad(final_tokens.reshape(band_rows, GRID_W, -1), ((0, 0), (1, 1), (0, 0)))
    window = lax.dynamic_slice_in_dim(grid, tile_index * column_count, column_count + 2, axis=1)
    wide_map = (
        jnp.dot(
            window.reshape(band_rows * (column_count + 2), -1),
            reassemble_full,
            preferred_element_type=jnp.float32,
        )
        .astype(jnp.bfloat16)
        .reshape(band_rows, column_count + 2, CH)
    )
    feature_map = wide_map[:, 1 : column_count + 1]
    activated = jnp.maximum(wide_map, jnp.zeros((), jnp.bfloat16))
    padded = padded_2(activated, (("blk", 0),), 1)
    stacked = jnp.concatenate(
        [
            padded[row_shift : row_shift + band_rows, col_shift : col_shift + column_count]
            for row_shift in range(3)
            for col_shift in range(3)
        ],
        axis=-1,
    )
    convolved = jnp.dot(
        stacked.reshape(band_rows * column_count, 9 * CH),
        conv_weight.reshape(9 * CH, CH),
        preferred_element_type=jnp.float32,
    )
    joined = (
        feature_map.astype(jnp.float32) + convolved.reshape(band_rows, column_count, CH)
    ).astype(jnp.bfloat16)
    return joined[None]


def solution(mesh):
    placed = (
        P(("groups", "pair"), "blk", "tile"),
        P(("groups", "pair"), "blk", "tile"),
        P(None, None, "tile"),
        P("tile", None),
        P(None, None, "tile"),
        P("tile", None),
        P("tile", None),
        P(),
    )
    return jax.shard_map(
        body,
        mesh=mesh,
        in_specs=placed,
        out_specs=P(("groups", "pair"), "blk", "tile", None),
        check_vma=False,
    )
```

```python
import jax
import jax.numpy as jnp
from jax import lax
from jax.sharding import PartitionSpec as P

HD = 64
CH = 256
GRID_W = 128


def padded_2(cells, sides, width):
    for axis, dim in sides:
        count = lax.axis_size(axis)
        ends = count - 1
        head = lax.slice_in_dim(cells, 0, width, axis=dim)
        tail = lax.slice_in_dim(cells, cells.shape[dim] - width, cells.shape[dim], axis=dim)
        cells = jnp.concatenate(
            [
                lax.ppermute(tail, axis, [(i, (i + 1) % count) for i in range(ends)]),
                cells,
                lax.ppermute(head, axis, [((i + 1) % count, i) for i in range(ends)]),
            ],
            axis=dim,
        )
    return cells


def layer_norm(values):
    widened = values.astype(jnp.float32)
    centred = widened - jnp.mean(widened, axis=-1, keepdims=True)
    variance = jnp.mean(centred * centred, axis=-1, keepdims=True)
    return (centred * lax.rsqrt(variance + 1e-06)).astype(jnp.bfloat16)


def project_rows(normed, weight):
    return jnp.dot(normed, weight, preferred_element_type=jnp.float32).astype(jnp.bfloat16)


def initial_state(queries):
    query_count = queries.shape[0]
    head_count = queries.shape[1] // HD
    return (
        jnp.full((head_count, query_count), -1e30, jnp.float32),
        jnp.zeros((head_count, query_count), jnp.float32),
        jnp.zeros(queries.shape, jnp.float32),
    )


def attend_keys(running, queries, keys_rows, values_rows):
    maxima, totals, accumulated = running
    query_count = queries.shape[0]
    head_count = queries.shape[1] // HD
    key_count = keys_rows.shape[0]
    scores = jnp.einsum(
        "qhd,khd->hqk",
        queries.reshape(query_count, head_count, HD),
        keys_rows.reshape(key_count, head_count, HD),
        preferred_element_type=jnp.float32,
    ) * HD ** (-0.5)
    new_maxima = jnp.maximum(maxima, jnp.max(scores, axis=2))
    correction = jnp.exp(maxima - new_maxima)
    expanded = jnp.exp(scores - new_maxima[:, :, None])
    totals = totals * correction + jnp.sum(expanded, axis=2)
    mixed = jnp.einsum(
        "hqk,khd->qhd",
        expanded.astype(jnp.bfloat16),
        values_rows.reshape(key_count, head_count, HD),
        preferred_element_type=jnp.float32,
    )
    accumulated = (
        accumulated.reshape(query_count, head_count, HD) * correction.T[:, :, None] + mixed
    )
    return (new_maxima, totals, accumulated.reshape(query_count, head_count * HD))


def fold_keys(running, queries, keys_rows, values_rows):
    key_count = keys_rows.shape[0]
    block_rows = max((divisor for divisor in range(1, 1025) if key_count % divisor == 0))
    if block_rows == key_count:
        return attend_keys(running, queries, keys_rows, values_rows)
    stacked_keys = keys_rows.reshape(key_count // block_rows, block_rows, keys_rows.shape[1])
    stacked_values = values_rows.reshape(key_count // block_rows, block_rows, values_rows.shape[1])

    def step_block(current, blocks):
        return (attend_keys(current, queries, blocks[0], blocks[1]), None)

    result, unused = lax.scan(step_block, running, (stacked_keys, stacked_values))
    return result


def finish_state(running):
    maxima, totals, accumulated = running
    query_count = accumulated.shape[0]
    head_count = accumulated.shape[1] // HD
    normalized = accumulated.reshape(query_count, head_count, HD) / totals.T[:, :, None]
    return normalized.reshape(query_count, head_count * HD).astype(jnp.bfloat16)


def shifted(value, axis):
    count = lax.axis_size(axis)
    return [value] + [
        lax.ppermute(value, axis, [(i, (i + shift) % count) for i in range(count)])
        for shift in range(1, count)
    ]


def gather_ordered(value, axis):
    count = lax.axis_size(axis)
    stack = jnp.stack(shifted(value, axis))
    order = (lax.axis_index(axis) - jnp.arange(count)) % count
    return jnp.take(stack, order, axis=0)


def sum_over(value, axis):
    total = value.astype(jnp.float32)
    for piece in shifted(value, axis)[1:]:
        total = total + piece.astype(jnp.float32)
    return total


def body(
    left_tokens, right_tokens, self_qkv, self_out, cross_qkv, cross_out, reassemble, conv_weight
):
    tiles = lax.axis_size("tile")
    tile_index = lax.axis_index("tile")
    token_count, feature_share = left_tokens.shape[1], left_tokens.shape[2]
    tokens = gather_ordered(jnp.stack([left_tokens[0], right_tokens[0]]), "tile")
    left_full, right_full = (
        jnp.moveaxis(tokens[:, side], 0, 1).reshape(token_count, tiles * feature_share)
        for side in range(2)
    )
    reassemble_full = gather_ordered(reassemble, "tile").reshape(-1, CH)
    left_normed = layer_norm(left_full)
    right_normed = layer_norm(right_full)
    self_query = project_rows(left_normed, self_qkv[0])
    self_pieces = shifted(
        jnp.stack([project_rows(left_normed, self_qkv[1]), project_rows(left_normed, self_qkv[2])]),
        "blk",
    )
    cross_pieces = shifted(
        jnp.stack([project_rows(right_normed, cross_qkv[1]), project_rows(right_normed, cross_qkv[2])]),
        "blk",
    )
    self_state = initial_state(self_query)
    for piece in self_pieces:
        self_state = attend_keys(self_state, self_query, piece[0], piece[1])
    self_mixed = finish_state(self_state)
    self_term = jnp.dot(self_mixed, self_out, preferred_element_type=jnp.float32)
    self_sum = sum_over(self_term.astype(jnp.bfloat16), "tile")
    updated = (left_full.astype(jnp.float32) + self_sum).astype(jnp.bfloat16)
    updated_normed = layer_norm(updated)
    cross_query = project_rows(updated_normed, cross_qkv[0])
    cross_state = initial_state(cross_query)
    for piece in cross_pieces:
        cross_state = attend_keys(cross_state, cross_query, piece[0], piece[1])
    cross_mixed = finish_state(cross_state)
    cross_term = jnp.dot(cross_mixed, cross_out, preferred_element_type=jnp.float32)
    cross_sum = sum_over(cross_term.astype(jnp.bfloat16), "tile")
    final_tokens = (updated.astype(jnp.float32) + cross_sum).astype(jnp.bfloat16)
    band_rows = token_count // GRID_W
    column_count = GRID_W // tiles
    grid = jnp.pad(final_tokens.reshape(band_rows, GRID_W, -1), ((0, 0), (1, 1), (0, 0)))
    window = lax.dynamic_slice_in_dim(grid, tile_index * column_count, column_count + 2, axis=1)
    wide_map = (
        jnp.dot(
            window.reshape(band_rows * (column_count + 2), -1),
            reassemble_full,
            preferred_element_type=jnp.float32,
        )
        .astype(jnp.bfloat16)
        .reshape(band_rows, column_count + 2, CH)
    )
    feature_map = wide_map[:, 1 : column_count + 1]
    activated = jnp.maximum(wide_map, jnp.zeros((), jnp.bfloat16))
    padded = padded_2(activated, (("blk", 0),), 1)
    stacked = jnp.concatenate(
        [
            padded[row_shift : row_shift + band_rows, col_shift : col_shift + column_count]
            for row_shift in range(3)
            for col_shift in range(3)
        ],
        axis=-1,
    )
    convolved = jnp.dot(
        stacked.reshape(band_rows * column_count, 9 * CH),
        conv_weight.reshape(9 * CH, CH),
        preferred_element_type=jnp.float32,
    )
    joined = (
        feature_map.astype(jnp.float32) + convolved.reshape(band_rows, column_count, CH)
    ).astype(jnp.bfloat16)
    return joined[None]


def solution(mesh):
    placed = (
        P(("groups", "pair"), "blk", "tile"),
        P(("groups", "pair"), "blk", "tile"),
        P(None, None, "tile"),
        P("tile", None),
        P(None, None, "tile"),
        P("tile", None),
        P("tile", None),
        P(),
    )
    return jax.shard_map(
        body,
        mesh=mesh,
        in_specs=placed,
        out_specs=P(("groups", "pair"), "blk", "tile", None),
        check_vma=False,
    )
```

```python
import jax
import jax.numpy as jnp
from jax import lax
from jax.sharding import PartitionSpec as P

HD = 64
CH = 256
GRID_W = 128


def padded_2(cells, sides, width):
    for axis, dim in sides:
        count = lax.axis_size(axis)
        ends = count - 1
        head = lax.slice_in_dim(cells, 0, width, axis=dim)
        tail = lax.slice_in_dim(cells, cells.shape[dim] - width, cells.shape[dim], axis=dim)
        cells = jnp.concatenate(
            [
                lax.ppermute(tail, axis, [(i, (i + 1) % count) for i in range(ends)]),
                cells,
                lax.ppermute(head, axis, [((i + 1) % count, i) for i in range(ends)]),
            ],
            axis=dim,
        )
    return cells


def layer_norm(values):
    widened = values.astype(jnp.float32)
    centred = widened - jnp.mean(widened, axis=-1, keepdims=True)
    variance = jnp.mean(centred * centred, axis=-1, keepdims=True)
    return (centred * lax.rsqrt(variance + 1e-06)).astype(jnp.bfloat16)


def project_rows(normed, weight):
    return jnp.dot(normed, weight, preferred_element_type=jnp.float32).astype(jnp.bfloat16)


def initial_state(queries):
    query_count = queries.shape[0]
    head_count = queries.shape[1] // HD
    return (
        jnp.full((head_count, query_count), -1e30, jnp.float32),
        jnp.zeros((head_count, query_count), jnp.float32),
        jnp.zeros(queries.shape, jnp.float32),
    )


def attend_keys(running, queries, keys_rows, values_rows):
    maxima, totals, accumulated = running
    query_count = queries.shape[0]
    head_count = queries.shape[1] // HD
    key_count = keys_rows.shape[0]
    scores = jnp.einsum(
        "qhd,khd->hqk",
        queries.reshape(query_count, head_count, HD),
        keys_rows.reshape(key_count, head_count, HD),
        preferred_element_type=jnp.float32,
    ) * HD ** (-0.5)
    new_maxima = jnp.maximum(maxima, jnp.max(scores, axis=2))
    correction = jnp.exp(maxima - new_maxima)
    expanded = jnp.exp(scores - new_maxima[:, :, None])
    totals = totals * correction + jnp.sum(expanded, axis=2)
    mixed = jnp.einsum(
        "hqk,khd->qhd",
        expanded.astype(jnp.bfloat16),
        values_rows.reshape(key_count, head_count, HD),
        preferred_element_type=jnp.float32,
    )
    accumulated = (
        accumulated.reshape(query_count, head_count, HD) * correction.T[:, :, None] + mixed
    )
    return (new_maxima, totals, accumulated.reshape(query_count, head_count * HD))


def fold_keys(running, queries, keys_rows, values_rows):
    key_count = keys_rows.shape[0]
    block_rows = max((divisor for divisor in range(1, 1025) if key_count % divisor == 0))
    if block_rows == key_count:
        return attend_keys(running, queries, keys_rows, values_rows)
    stacked_keys = keys_rows.reshape(key_count // block_rows, block_rows, keys_rows.shape[1])
    stacked_values = values_rows.reshape(key_count // block_rows, block_rows, values_rows.shape[1])

    def step_block(current, blocks):
        return (attend_keys(current, queries, blocks[0], blocks[1]), None)

    result, unused = lax.scan(step_block, running, (stacked_keys, stacked_values))
    return result


def finish_state(running):
    maxima, totals, accumulated = running
    query_count = accumulated.shape[0]
    head_count = accumulated.shape[1] // HD
    normalized = accumulated.reshape(query_count, head_count, HD) / totals.T[:, :, None]
    return normalized.reshape(query_count, head_count * HD).astype(jnp.bfloat16)


def shifted(value, axis):
    count = lax.axis_size(axis)
    return [value] + [
        lax.ppermute(value, axis, [(i, (i + shift) % count) for i in range(count)])
        for shift in range(1, count)
    ]


def gather_ordered(value, axis):
    count = lax.axis_size(axis)
    stack = jnp.stack(shifted(value, axis))
    order = (lax.axis_index(axis) - jnp.arange(count)) % count
    return jnp.take(stack, order, axis=0)


def sum_over(value, axis):
    total = value.astype(jnp.float32)
    for piece in shifted(value, axis)[1:]:
        total = total + piece.astype(jnp.float32)
    return total


def body(
    left_tokens, right_tokens, self_qkv, self_out, cross_qkv, cross_out, reassemble, conv_weight
):
    tiles = lax.axis_size("tile")
    tile_index = lax.axis_index("tile")
    token_count, feature_share = left_tokens.shape[1], left_tokens.shape[2]
    left_full, right_full = (
        jnp.moveaxis(gather_ordered(side[0], "tile"), 0, 1).reshape(token_count, tiles * feature_share)
        for side in (left_tokens, right_tokens)
    )
    reassemble_full = gather_ordered(reassemble, "tile").reshape(-1, CH)
    left_normed = layer_norm(left_full)
    right_normed = layer_norm(right_full)
    self_query = project_rows(left_normed, self_qkv[0])
    self_pieces = shifted(
        jnp.stack([project_rows(left_normed, self_qkv[1]), project_rows(left_normed, self_qkv[2])]),
        "blk",
    )
    cross_pieces = shifted(
        jnp.stack([project_rows(right_normed, cross_qkv[1]), project_rows(right_normed, cross_qkv[2])]),
        "blk",
    )
    self_state = initial_state(self_query)
    for piece in self_pieces:
        self_state = attend_keys(self_state, self_query, piece[0], piece[1])
    self_mixed = finish_state(self_state)
    self_term = jnp.dot(self_mixed, self_out, preferred_element_type=jnp.float32)
    self_sum = sum_over(self_term.astype(jnp.bfloat16), "tile")
    updated = (left_full.astype(jnp.float32) + self_sum).astype(jnp.bfloat16)
    updated_normed = layer_norm(updated)
    cross_query = project_rows(updated_normed, cross_qkv[0])
    cross_state = initial_state(cross_query)
    for piece in cross_pieces:
        cross_state = attend_keys(cross_state, cross_query, piece[0], piece[1])
    cross_mixed = finish_state(cross_state)
    cross_term = jnp.dot(cross_mixed, cross_out, preferred_element_type=jnp.float32)
    cross_sum = sum_over(cross_term.astype(jnp.bfloat16), "tile")
    final_tokens = (updated.astype(jnp.float32) + cross_sum).astype(jnp.bfloat16)
    band_rows = token_count // GRID_W
    column_count = GRID_W // tiles
    grid = jnp.pad(final_tokens.reshape(band_rows, GRID_W, -1), ((0, 0), (1, 1), (0, 0)))
    window = lax.dynamic_slice_in_dim(grid, tile_index * column_count, column_count + 2, axis=1)
    wide_map = (
        jnp.dot(
            window.reshape(band_rows * (column_count + 2), -1),
            reassemble_full,
            preferred_element_type=jnp.float32,
        )
        .astype(jnp.bfloat16)
        .reshape(band_rows, column_count + 2, CH)
    )
    feature_map = wide_map[:, 1 : column_count + 1]
    activated = jnp.maximum(wide_map, jnp.zeros((), jnp.bfloat16))
    padded = padded_2(activated, (("blk", 0),), 1)
    stacked = jnp.concatenate(
        [
            padded[row_shift : row_shift + band_rows, col_shift : col_shift + column_count]
            for row_shift in range(3)
            for col_shift in range(3)
        ],
        axis=-1,
    )
    convolved = jnp.dot(
        stacked.reshape(band_rows * column_count, 9 * CH),
        conv_weight.reshape(9 * CH, CH),
        preferred_element_type=jnp.float32,
    )
    joined = (
        feature_map.astype(jnp.float32) + convolved.reshape(band_rows, column_count, CH)
    ).astype(jnp.bfloat16)
    return joined[None]


def solution(mesh):
    placed = (
        P(("groups", "pair"), "blk", "tile"),
        P(("groups", "pair"), "blk", "tile"),
        P(None, None, "tile"),
        P("tile", None),
        P(None, None, "tile"),
        P("tile", None),
        P("tile", None),
        P(),
    )
    return jax.shard_map(
        body,
        mesh=mesh,
        in_specs=placed,
        out_specs=P(("groups", "pair"), "blk", "tile", None),
        check_vma=False,
    )
```
